1024 devices in a mesh: group: 64 (over x, z), head: 8 (over y_hi, core), hid: 2 (over y_lo).
Axes of the slice: x: 4, y: 8 (y_hi: 4, y_lo: 2; y = y_hi * 2 + y_lo), z: 16, core: 2. Of those that a mesh axis runs over, the one named last changes fastest.
Arguments:
- tokens: bfloat16 [16384, 5120], P(('group', 'head', 'hid')), may hold values from -6 to 6
- w_query: bfloat16 [5120, 4096], P('group', ('head', 'hid')), may hold values from -0.078125 to 0.078125
- keyval_weight: bfloat16 [5120, 8, 256], P(('group', 'hid'), 'head'), may hold values from -0.078125 to 0.078125
- q_gain: float32 [128], replicated, may hold values from 0.1 to 1.9
- k_gain: float32 [128], replicated, may hold values from 0.1 to 1.9
- segments: int32 [64, 256], P('group'), may hold values from 0 to 3, never falling along the last dimension, each value on 1 to 128 neighbouring positions
Outputs:
- attention: bfloat16 [16384, 4096], P('group', ('head', 'hid'))
- kv_cache: bfloat16 [16384, 8, 256], P('group', 'head')
The draws below stay inside these ranges and needn't reach their ends.
Inputs may be any that keep to these rules, and one draw needn't show every extreme that they name: `segments`: within each replica's 256 tokens segment numbers never fall; each of the 4 sequences holds 1 to 128 tokens and one holds exactly 128.
All inputs are finite; a program needn't handle non-finite values.
Results may differ from the reference program's by a relative error of at most 0.0068.
Values may be sent and summed in bfloat16 or wider, within the bound.
No kernel may reach another device: no remote copies, remote signals or barrier semaphores. Data moves between devices by JAX's collectives and lax.ppermute only.
A program may use at most 32 MiB of HBM per device.

```python
import math
import jax
import jax.numpy as jnp
import numpy as np
from jax import lax

MODEL_WIDTH = 5120
QUERY_HEADS = 32
KEYVAL_HEADS = 8
HEAD_WIDTH = 128
TOK_G = 256
SEQS = 4
MOST = 128
TOKENS = 16384
N_GROUP = 64


def steps_of(rng, dims, split, least, top_value):
    level, own = 1.0, jax.random.fold_in(rng, 6)
    for position, parts in split:
        steps = jnp.exp(jax.random.uniform(jax.random.fold_in(own, position), (parts,), jnp.float32, least / len(split), top_value / len(split)))
        level = level * jnp.repeat(steps, dims[position] // parts).reshape([-1 if axis == position else 1 for axis in range(len(dims))])
    return level


def split_up(count, total, reach, slope):
    loads = [(1 << 20) // math.isqrt(standing ** slope) + 1 for standing in range(2, count + 1)]
    spare, counts = total - reach - (count - 1), [1] * (count - 1)
    while spare > 0:
        movable = [i for i in range(count - 1) if counts[i] < reach]
        whole, left = sum([loads[i] for i in movable]), spare
        for i in movable:
            more = min(reach - counts[i], max(1, left * loads[i] // whole), spare)
            counts[i] = counts[i] + more
            spare = spare - more
    return np.array([reach] + counts)


def uneven(stream_key, amount, total, limit, lean):
    if amount == 2:
        one = jax.random.randint(stream_key, (), max(1, total - limit), min(limit, total - 1) + 1)
        return jnp.stack([one, total - one])
    tallies = jnp.asarray(split_up(amount, total, limit, lean), jnp.int32)
    twos = (amount - 1) // 2
    donor, sink = tallies[1:1 + 2 * twos:2], tallies[2:2 + 2 * twos:2]
    room = jnp.minimum(donor - 1, limit - sink)
    passed = jax.random.randint(jax.random.fold_in(stream_key, 1), (twos,), 0, 1 << 20) % (room + 1)
    tallies = tallies.at[1:1 + 2 * twos:2].set(donor - passed).at[2:2 + 2 * twos:2].set(sink + passed)
    return tallies[jax.random.permutation(jax.random.fold_in(stream_key, 2), amount)]


def noise(rng, shape, deviation, most, pieces=(), kind=jnp.bfloat16):
    drawn = jax.random.normal(rng, shape, jnp.float32) * deviation
    if len(pieces) > 0:
        drawn = steps_of(rng, shape, pieces, -0.22, 0.18) * drawn
    return jnp.clip(drawn, min=-most, max=most).astype(kind)


def setup_inputs(seed: int = 0) -> dict:
    key_of = jax.random.split(jax.random.key(seed), 7)
    tokens = noise(key_of[0], (TOKENS, MODEL_WIDTH), 1.0, 6.0, ((0, 1024),))
    w_query = noise(key_of[1], (MODEL_WIDTH, QUERY_HEADS * HEAD_WIDTH), MODEL_WIDTH ** -0.5, 0.078125, ((0, 64), (1, 16)))
    keyval_weight = noise(key_of[2], (MODEL_WIDTH, KEYVAL_HEADS, 2 * HEAD_WIDTH), MODEL_WIDTH ** -0.5, 0.078125, ((0, 128), (1, 8)))
    q_gain = jnp.clip(1.0 + 0.18 * jax.random.normal(key_of[3], (HEAD_WIDTH,), jnp.float32), 0.1, 1.9)
    k_gain = jnp.clip(1.0 + 0.18 * jax.random.normal(key_of[4], (HEAD_WIDTH,), jnp.float32), 0.1, 1.9)
    segments = jax.vmap(lambda own: jnp.searchsorted(jnp.cumsum(uneven(own, SEQS, TOK_G, MOST, 1)), jnp.arange(TOK_G), side="right"))(jax.random.split(key_of[5], N_GROUP)).reshape((N_GROUP, TOK_G)).astype(jnp.int32)
    return dict(tokens=tokens, w_query=w_query, keyval_weight=keyval_weight, q_gain=q_gain, k_gain=k_gain, segments=segments)


theta_base = 1000000.0
epsilon = 1e-06

def head_norm(values, gain):
    return values * lax.rsqrt(lax.optimization_barrier(jnp.mean(values * values, axis=-1, keepdims=True)) + epsilon) * gain

def rotate(values, places):
    width = values.shape[-1]
    half = width // 2
    index = jnp.arange(half, dtype=jnp.float32)
    freqs = jnp.power(theta_base, -2.0 * index / width)
    angles = places.astype(jnp.float32)[:, None] * freqs[None, :]
    cosine = jnp.cos(angles)[:, None, :]
    sine = jnp.sin(angles)[:, None, :]
    first_half = values[..., :half]
    second_half = values[..., half:]
    return jnp.concatenate([first_half * cosine - second_half * sine, second_half * cosine + first_half * sine], axis=-1)

def token_places(seg_ids):
    count_total = seg_ids.shape[0]
    before = lax.optimization_barrier(jnp.sum((seg_ids[None, :] < seg_ids[:, None]).astype(jnp.int32), axis=1))
    return jnp.arange(count_total, dtype=jnp.int32) - before

def reference(tokens, w_query, keyval_weight, q_gain, k_gain, segments):
    groups = segments.shape[0]
    group_ratio = QUERY_HEADS // KEYVAL_HEADS

    def one_group(inputs):
        block_tile, seg_ids = inputs
        count_total = block_tile.shape[0]
        places = token_places(seg_ids)
        query = jnp.dot(block_tile, w_query, preferred_element_type=jnp.float32).reshape(count_total, QUERY_HEADS, HEAD_WIDTH)
        key_value = jnp.dot(block_tile, keyval_weight.reshape(MODEL_WIDTH, KEYVAL_HEADS * 2 * HEAD_WIDTH), preferred_element_type=jnp.float32).reshape(count_total, KEYVAL_HEADS, 2 * HEAD_WIDTH)
        key_rot = rotate(head_norm(key_value[..., :HEAD_WIDTH], k_gain), places).astype(jnp.bfloat16)
        value_b = key_value[..., HEAD_WIDTH:].astype(jnp.bfloat16)
        cache_store = jnp.concatenate([key_rot, value_b], axis=-1)
        query_rot = rotate(head_norm(query, q_gain), places).astype(jnp.bfloat16)
        key_all = jnp.repeat(key_rot, group_ratio, axis=1)
        value_all = jnp.repeat(value_b, group_ratio, axis=1)
        scores = jnp.einsum('qhd,khd->hqk', query_rot.astype(jnp.float32), key_all.astype(jnp.float32)) / jnp.sqrt(jnp.float32(HEAD_WIDTH))
        index = jnp.arange(count_total, dtype=jnp.int32)
        allowed = (index[None, :] <= index[:, None]) & (seg_ids[None, :] == seg_ids[:, None])
        masked = jnp.where(allowed[None], scores, jnp.float32(-1e+30))
        peak = lax.optimization_barrier(jnp.max(masked, axis=-1, keepdims=True))
        expd = jnp.where(allowed[None], jnp.exp(masked - peak), jnp.float32(0.0))
        probs = (expd / lax.optimization_barrier(jnp.sum(expd, axis=-1, keepdims=True))).astype(jnp.bfloat16)
        output = jnp.einsum('hqk,khd->qhd', probs.astype(jnp.float32), value_all.astype(jnp.float32))
        return (output.astype(jnp.bfloat16).reshape(count_total, QUERY_HEADS * HEAD_WIDTH), cache_store)
    attention, cache_store = lax.map(one_group, (tokens.reshape(groups, -1, MODEL_WIDTH), segments))
    return (attention.reshape(-1, QUERY_HEADS * HEAD_WIDTH), cache_store.reshape(-1, KEYVAL_HEADS, 2 * HEAD_WIDTH))
```

```python
import jax
import jax.numpy as jnp
from jax import lax
from jax.sharding import Mesh, PartitionSpec as P

QUERY_HEADS = 32
KEYVAL_HEADS = 8

theta_base = 1000000.0
epsilon = 1e-06

N_X, N_Z, N_YH, N_CORE, N_YL = 4, 16, 4, 2, 2


def head_norm(values, gain):
    return values * lax.rsqrt(jnp.mean(values * values, axis=-1, keepdims=True) + epsilon) * gain


def rotate(values, cosine, sine):
    half = values.shape[-1] // 2
    first_half = values[..., :half]
    second_half = values[..., half:]
    return jnp.concatenate(
        [first_half * cosine - second_half * sine, second_half * cosine + first_half * sine],
        axis=-1,
    )


def token_places(seg_ids):
    count_total = seg_ids.shape[0]
    before = jnp.sum((seg_ids[None, :] < seg_ids[:, None]).astype(jnp.int32), axis=1)
    return jnp.arange(count_total, dtype=jnp.int32) - before


def attend(query_rot, key_rot, value_b, seg_ids):
    count_total = query_rot.shape[0]
    width = query_rot.shape[-1]
    scores = jnp.einsum(
        "qhd,kd->hqk", query_rot, key_rot, preferred_element_type=jnp.float32
    ) / jnp.sqrt(jnp.float32(width))
    index = jnp.arange(count_total, dtype=jnp.int32)
    allowed = (index[None, :] <= index[:, None]) & (seg_ids[None, :] == seg_ids[:, None])
    masked = jnp.where(allowed[None], scores, jnp.float32(-1e30))
    peak = jnp.max(masked, axis=-1, keepdims=True)
    expd = jnp.where(allowed[None], jnp.exp(masked - peak), jnp.float32(0.0))
    probs = (expd / jnp.sum(expd, axis=-1, keepdims=True)).astype(jnp.bfloat16)
    output = jnp.einsum("hqk,kd->qhd", probs, value_b, preferred_element_type=jnp.float32)
    return output.astype(jnp.bfloat16).reshape(count_total, -1)


def body(tokens, w_query, keyval_weight, q_gain, k_gain, segments):
    q_rows, q_cols = w_query.shape
    kv_rows, _, pair_width = keyval_weight.shape
    head_size = pair_width // 2
    near = lax.axis_index("yl")

    whole = lax.all_gather(tokens, ("yh", "core", "yl"), axis=0, tiled=True)

    block = jnp.concatenate([w_query, keyval_weight.reshape(kv_rows, pair_width)], axis=0)
    column = lax.all_gather(block, "z", axis=0)
    plane = lax.all_to_all(
        jnp.broadcast_to(column[None], (N_X, *column.shape)), "x", split_axis=0, concat_axis=0
    ).reshape(N_X * N_Z, q_rows + kv_rows, q_cols)
    wq = plane[:, :q_rows].reshape(-1, q_cols)
    wkv = lax.dynamic_update_slice(
        jnp.zeros((N_X * N_Z, N_YL * kv_rows, pair_width), jnp.bfloat16),
        plane[:, q_rows:],
        (0, near * kv_rows, 0),
    ).reshape(-1, pair_width)

    def product(weight):
        return jnp.dot(whole, weight, preferred_element_type=jnp.float32)

    partial = product(wkv)
    key_value = partial + lax.ppermute(partial, "yl", [(0, 1), (1, 0)])
    query = product(wq)
    count_total = query.shape[0]

    seg_ids = segments.reshape(-1)
    places = token_places(seg_ids)
    half = head_size // 2
    freqs = jnp.power(theta_base, -2.0 * jnp.arange(half, dtype=jnp.float32) / head_size)
    angles = places.astype(jnp.float32)[:, None] * freqs[None, :]
    cosine, sine = jnp.cos(angles), jnp.sin(angles)
    key_rot = rotate(head_norm(key_value[:, :head_size], k_gain), cosine, sine).astype(jnp.bfloat16)
    value_b = key_value[:, head_size:].astype(jnp.bfloat16)
    cache_store = jnp.concatenate([key_rot, value_b], axis=-1)[:, None, :]
    query_rot = rotate(
        head_norm(query.reshape(count_total, -1, head_size), q_gain), cosine[:, None, :], sine[:, None, :]
    ).astype(jnp.bfloat16)
    return (attend(query_rot, key_rot, value_b, seg_ids), cache_store)


def solution(mesh):
    fine = Mesh(
        mesh.devices.reshape(N_X, N_Z, N_YH, N_CORE, N_YL), ("x", "z", "yh", "core", "yl")
    )
    group, head = ("x", "z"), ("yh", "core")
    return jax.shard_map(
        body,
        mesh=fine,
        in_specs=(
            P((*group, *head, "yl"), None),
            P(group, (*head, "yl")),
            P((*group, "yl"), head, None),
            P(),
            P(),
            P(group, None),
        ),
        out_specs=(P(group, (*head, "yl")), P(group, head, None)),
        check_vma=False,
    )
```

```python
import functools
import math

import jax
import jax.numpy as jnp
from jax import lax
from jax.experimental import pallas as pl
from jax.experimental.pallas import tpu as pltpu
from jax.sharding import Mesh, PartitionSpec as P

QUERY_HEADS = 32
KEYVAL_HEADS = 8

theta_base = 1000000.0
epsilon = 1e-06

N_X, N_Z, N_YH, N_CORE, N_YL = 4, 16, 4, 2, 2
VMEM = pl.BlockSpec(memory_space=pltpu.VMEM)
HBM = pl.BlockSpec(memory_space=pltpu.HBM)


def token_places(seg_ids):
    count_total = seg_ids.shape[0]
    before = jnp.sum((seg_ids[None, :] < seg_ids[:, None]).astype(jnp.int32), axis=1)
    return jnp.arange(count_total, dtype=jnp.int32) - before


def norm_rotate(values, gain, cosine, sine):
    mean = jnp.mean(values * values, axis=-1, keepdims=True)
    values = values * lax.rsqrt(mean + epsilon) * gain
    return values * cosine + pltpu.roll(values, values.shape[-1] // 2, 1) * sine


def meet(where, held, steps, weight):
    rows = weight.reshape(-1, weight.shape[-1])
    wide = rows.shape[0]
    start = pl.multiple_of(lax.rem(where[0] + steps, N_X) * wide, wide)
    return jnp.dot(
        held[:, :, :, :, pl.ds(start, wide)].reshape(-1, wide), rows, preferred_element_type=jnp.float32
    )


def order_kernel(whole, held, sems):
    copies = [
        pltpu.make_async_copy(whole.at[:, near, core], held.at[:, core, near], sems.at[core, near])
        for core in range(N_CORE)
        for near in range(N_YL)
    ]
    for copy in copies:
        copy.start()
    for copy in copies:
        copy.wait()


def keyval_kernel(where, held, own, right, left, far, out, weight):
    rows = own.shape[1]
    for half in range(N_YL):

        @pl.when(where[1] == half)
        def _():
            away = (1 - half) * rows
            for n, ref in enumerate((own, left, far, right)):
                weight[n, :, half * rows : half * rows + rows, :] = ref[...]
                weight[n, :, away : away + rows, :] = jnp.zeros_like(ref)

    out[...] = sum(meet(where, held, n, weight[n]) for n in range(N_X))


def query_kernel(where, held, own, right, left, out):
    out[...] = (
        meet(where, held, 0, own[...]) + meet(where, held, N_X - 1, right[...]) + meet(where, held, 1, left[...])
    )


def attend_kernel(head_size, where, held, far, near, own, partner, q_gain, k_gain, cosine, sine, bias, out, cache):
    query = near[...] + meet(where, held, 2, far[...])
    key_value = own[...] + partner[...]
    key_rot = norm_rotate(key_value[:, :head_size], k_gain[...], cosine[...], sine[...]).astype(jnp.bfloat16)
    value_b = key_value[:, head_size:].astype(jnp.bfloat16)
    cache[:, :head_size] = key_rot
    cache[:, head_size:] = value_b
    for h in range(out.shape[1] // head_size):
        span = slice(h * head_size, (h + 1) * head_size)
        query_rot = norm_rotate(query[:, span], q_gain[...], cosine[...], sine[...]).astype(jnp.bfloat16)
        scores = lax.dot_general(
            query_rot, key_rot, (((1,), (1,)), ((), ())), preferred_element_type=jnp.float32
        ) / math.sqrt(head_size)
        masked = scores + bias[...]
        expd = jnp.exp(masked - jnp.max(masked, axis=-1, keepdims=True))
        probs = (expd / jnp.sum(expd, axis=-1, keepdims=True)).astype(jnp.bfloat16)
        out[:, span] = jnp.dot(probs, value_b, preferred_element_type=jnp.float32).astype(jnp.bfloat16)


def body(tokens, w_query, keyval_weight, q_gain, k_gain, segments):
    q_rows, q_cols = w_query.shape
    kv_rows, _, pair_width = keyval_weight.shape
    head_size = pair_width // 2
    where = jnp.stack([lax.axis_index(axis) for axis in ("x", "yl")]).astype(jnp.int32)

    pair = lax.all_gather(tokens, "core", axis=0, tiled=True)
    whole = lax.all_gather(pair, ("yh", "yl"), axis=0, tiled=True)

    seg_ids = segments.reshape(-1)
    count_total = seg_ids.shape[0]
    half = head_size // 2
    freqs = jnp.power(theta_base, -2.0 * jnp.arange(half, dtype=jnp.float32) / head_size)
    angles = token_places(seg_ids).astype(jnp.float32)[:, None] * freqs[None, :]
    cosine, sine = jnp.cos(angles), jnp.sin(angles)
    cosine = jnp.concatenate([cosine, cosine], axis=1)
    sine = jnp.concatenate([-sine, sine], axis=1)

    index = jnp.arange(count_total, dtype=jnp.int32)
    allowed = (index[None, :] <= index[:, None]) & (seg_ids[None, :] == seg_ids[:, None])
    bias = jnp.where(allowed, jnp.float32(0.0), jnp.float32(-1e30))

    block = jnp.concatenate([w_query, keyval_weight.reshape(kv_rows, pair_width)], axis=0)
    column = lax.all_gather(block, "z", axis=0)
    query_own, key_own = column[:, :q_rows], column[:, q_rows:]

    def up(a):
        return lax.ppermute(a, "x", [(x, (x + 1) % N_X) for x in range(N_X)])

    def down(a):
        return lax.ppermute(a, "x", [(x, (x - 1) % N_X) for x in range(N_X)])

    key_right, query_left = up(key_own), down(query_own)
    query_right, key_left = up(query_own), down(key_own)
    key_right, where, cosine, sine, bias = lax.optimization_barrier((key_right, where, cosine, sine, bias))
    key_far, query_far = up(key_right), down(query_left)
    query_right, key_left, key_right, whole = lax.optimization_barrier((query_right, key_left, key_right, whole))
    depth = N_X * N_Z * q_rows
    held = pl.pallas_call(
        order_kernel,
        out_shape=jax.ShapeDtypeStruct((N_YH, N_CORE, N_YL, tokens.shape[0], depth), jnp.bfloat16),
        in_specs=[HBM],
        out_specs=VMEM,
        scratch_shapes=[pltpu.SemaphoreType.DMA((N_CORE, N_YL))],
        cost_estimate=pl.CostEstimate(flops=0, bytes_accessed=4 * count_total * depth, transcendentals=0),
        compiler_params=pltpu.CompilerParams(vmem_limit_bytes=16 << 20),
    )(pltpu.with_memory_space_constraint(whole.reshape(N_YH, N_YL, N_CORE, tokens.shape[0], depth), pltpu.HBM))

    smem = pl.BlockSpec(memory_space=pltpu.SMEM)

    def settings(slots):
        return dict(
            cost_estimate=pl.CostEstimate(
                flops=2 * slots * count_total * (depth // N_X) * q_cols,
                bytes_accessed=2 * slots * (depth // N_X) * (q_cols + count_total),
                transcendentals=0,
            ),
            compiler_params=pltpu.CompilerParams(vmem_limit_bytes=16 << 20),
        )

    partial = pl.pallas_call(
        keyval_kernel,
        out_shape=jax.ShapeDtypeStruct((count_total, pair_width), jnp.float32),
        in_specs=[smem, *[VMEM] * 5],
        out_specs=VMEM,
        scratch_shapes=[pltpu.VMEM((N_X, N_Z, q_rows, q_cols), jnp.bfloat16)],
        **settings(N_X),
    )(where, held, key_own, key_right, key_left, key_far)
    partner = lax.ppermute(partial, "yl", [(0, 1), (1, 0)])
    near = pl.pallas_call(
        query_kernel,
        out_shape=jax.ShapeDtypeStruct((count_total, q_cols), jnp.float32),
        in_specs=[smem, *[VMEM] * 4],
        out_specs=VMEM,
        **settings(N_X - 1),
    )(where, held, query_own, query_right, query_left)
    attention, cache = pl.pallas_call(
        functools.partial(attend_kernel, head_size),
        out_shape=(
            jax.ShapeDtypeStruct((count_total, q_cols), jnp.bfloat16),
            jax.ShapeDtypeStruct((count_total, pair_width), jnp.bfloat16),
        ),
        in_specs=[smem, *[VMEM] * 10],
        out_specs=(VMEM, VMEM),
        **settings(1),
    )(where, held, query_far, near, partial, partner, q_gain[None], k_gain[None], cosine, sine, bias)
    return attention, cache[:, None, :]


def solution(mesh):
    fine = Mesh(
        mesh.devices.reshape(N_X, N_Z, N_YH, N_CORE, N_YL), ("x", "z", "yh", "core", "yl")
    )
    group, head = ("x", "z"), ("yh", "core")
    return jax.shard_map(
        body,
        mesh=fine,
        in_specs=(
            P((*group, *head, "yl"), None),
            P(group, (*head, "yl")),
            P((*group, "yl"), head, None),
            P(),
            P(),
            P(group, None),
        ),
        out_specs=(P(group, (*head, "yl")), P(group, head, None)),
        check_vma=False,
    )
```

```python
import functools
import math

import jax
import jax.numpy as jnp
from jax import lax
from jax.experimental import pallas as pl
from jax.experimental.pallas import tpu as pltpu
from jax.sharding import Mesh, PartitionSpec as P

QUERY_HEADS = 32
KEYVAL_HEADS = 8

theta_base = 1000000.0
epsilon = 1e-06

N_X, N_Z, N_YH, N_CORE, N_YL = 4, 16, 4, 2, 2
VMEM = pl.BlockSpec(memory_space=pltpu.VMEM)
HBM = pl.BlockSpec(memory_space=pltpu.HBM)


def token_places(seg_ids):
    count_total = seg_ids.shape[0]
    before = jnp.sum((seg_ids[None, :] < seg_ids[:, None]).astype(jnp.int32), axis=1)
    return jnp.arange(count_total, dtype=jnp.int32) - before


def norm_rotate(values, gain, cosine, sine):
    mean = jnp.mean(values * values, axis=-1, keepdims=True)
    values = values * lax.rsqrt(mean + epsilon) * gain
    return values * cosine + pltpu.roll(values, values.shape[-1] // 2, 1) * sine


def meet(where, held, steps, weight):
    rows = weight.reshape(-1, weight.shape[-1])
    wide = rows.shape[0]
    start = pl.multiple_of(lax.rem(where[0] + steps, N_X) * wide, wide)
    return jnp.dot(
        held[:, :, :, :, pl.ds(start, wide)].reshape(-1, wide), rows, preferred_element_type=jnp.float32
    )


def order_kernel(whole, held, sems):
    copies = [
        pltpu.make_async_copy(whole.at[:, near, core], held.at[:, core, near], sems.at[core, near])
        for core in range(N_CORE)
        for near in range(N_YL)
    ]
    for copy in copies:
        copy.start()
    for copy in copies:
        copy.wait()


def keyval_kernel(where, held, own, right, left, far, out, weight):
    rows = own.shape[1]
    for half in range(N_YL):

        @pl.when(where[1] == half)
        def _():
            away = (1 - half) * rows
            for n, ref in enumerate((own, left, far, right)):
                weight[n, :, half * rows : half * rows + rows, :] = ref[...]
                weight[n, :, away : away + rows, :] = jnp.zeros_like(ref)

    out[...] = sum(meet(where, held, n, weight[n]) for n in range(N_X))


def query_kernel(where, held, own, right, left, out):
    out[...] = (
        meet(where, held, 0, own[...]) + meet(where, held, N_X - 1, right[...]) + meet(where, held, 1, left[...])
    )


def attend_kernel(head_size, where, held, far, near, own, partner, q_gain, k_gain, cosine, sine, bias, out, cache):
    query = near[...] + meet(where, held, 2, far[...])
    key_value = own[...] + partner[...]
    key_rot = norm_rotate(key_value[:, :head_size], k_gain[...], cosine[...], sine[...]).astype(jnp.bfloat16)
    value_b = key_value[:, head_size:].astype(jnp.bfloat16)
    cache[:, :head_size] = key_rot
    cache[:, head_size:] = value_b
    for h in range(out.shape[1] // head_size):
        span = slice(h * head_size, (h + 1) * head_size)
        query_rot = norm_rotate(query[:, span], q_gain[...], cosine[...], sine[...]).astype(jnp.bfloat16)
        scores = lax.dot_general(
            query_rot, key_rot, (((1,), (1,)), ((), ())), preferred_element_type=jnp.float32
        ) / math.sqrt(head_size)
        masked = scores + bias[...]
        expd = jnp.exp(masked - jnp.max(masked, axis=-1, keepdims=True))
        probs = (expd / jnp.sum(expd, axis=-1, keepdims=True)).astype(jnp.bfloat16)
        out[:, span] = jnp.dot(probs, value_b, preferred_element_type=jnp.float32).astype(jnp.bfloat16)


def body(tokens, w_query, keyval_weight, q_gain, k_gain, segments):
    q_rows, q_cols = w_query.shape
    kv_rows, _, pair_width = keyval_weight.shape
    head_size = pair_width // 2
    where = jnp.stack([lax.axis_index(axis) for axis in ("x", "yl")]).astype(jnp.int32)

    pair = lax.all_gather(tokens, "core", axis=0, tiled=True)
    whole = lax.all_gather(pair, ("yh", "yl"), axis=0, tiled=True)

    seg_ids = segments.reshape(-1)
    count_total = seg_ids.shape[0]
    half = head_size // 2
    freqs = jnp.power(theta_base, -2.0 * jnp.arange(half, dtype=jnp.float32) / head_size)
    angles = token_places(seg_ids).astype(jnp.float32)[:, None] * freqs[None, :]
    cosine, sine = jnp.cos(angles), jnp.sin(angles)
    cosine = jnp.concatenate([cosine, cosine], axis=1)
    sine = jnp.concatenate([-sine, sine], axis=1)

    index = jnp.arange(count_total, dtype=jnp.int32)
    allowed = (index[None, :] <= index[:, None]) & (seg_ids[None, :] == seg_ids[:, None])
    bias = jnp.where(allowed, jnp.float32(0.0), jnp.float32(-1e30))

    block = jnp.concatenate([w_query, keyval_weight.reshape(kv_rows, pair_width)], axis=0)
    column = lax.all_gather(block, "z", axis=0)
    def up(a):
        return lax.ppermute(a, "x", [(x, (x + 1) % N_X) for x in range(N_X)])

    def down(a):
        return lax.ppermute(a, "x", [(x, (x - 1) % N_X) for x in range(N_X)])

    query_left = down(column[:, :q_rows])
    column, where, cosine, sine, bias = lax.optimization_barrier((column, where, cosine, sine, bias))
    key_own = column[:, q_rows:]
    key_right, key_left = up(key_own), down(key_own)
    column, key_right = lax.optimization_barrier((column, key_right))
    query_own = column[:, :q_rows]
    query_right = up(query_own)
    key_far = up(key_right)
    whole, key_right = lax.optimization_barrier((whole, key_right))
    depth = N_X * N_Z * q_rows
    held = pl.pallas_call(
        order_kernel,
        out_shape=jax.ShapeDtypeStruct((N_YH, N_CORE, N_YL, tokens.shape[0], depth), jnp.bfloat16),
        in_specs=[HBM],
        out_specs=VMEM,
        scratch_shapes=[pltpu.SemaphoreType.DMA((N_CORE, N_YL))],
        cost_estimate=pl.CostEstimate(flops=0, bytes_accessed=10 * 4 * count_total * depth, transcendentals=0),
        compiler_params=pltpu.CompilerParams(vmem_limit_bytes=16 << 20),
    )(pltpu.with_memory_space_constraint(whole.reshape(N_YH, N_YL, N_CORE, tokens.shape[0], depth), pltpu.HBM))

    query_left, held = lax.optimization_barrier((query_left, held))
    query_far = down(query_left)
    smem = pl.BlockSpec(memory_space=pltpu.SMEM)

    def settings(slots):
        return dict(
            cost_estimate=pl.CostEstimate(
                flops=10 * 2 * slots * count_total * (depth // N_X) * q_cols,
                bytes_accessed=10 * 2 * slots * (depth // N_X) * (q_cols + count_total),
                transcendentals=0,
            ),
            compiler_params=pltpu.CompilerParams(vmem_limit_bytes=16 << 20),
        )

    partial = pl.pallas_call(
        keyval_kernel,
        out_shape=jax.ShapeDtypeStruct((count_total, pair_width), jnp.float32),
        in_specs=[smem, *[VMEM] * 5],
        out_specs=VMEM,
        scratch_shapes=[pltpu.VMEM((N_X, N_Z, q_rows, q_cols), jnp.bfloat16)],
        **settings(N_X),
    )(where, held, key_own, key_right, key_left, key_far)
    partner = lax.ppermute(partial, "yl", [(0, 1), (1, 0)])
    near = pl.pallas_call(
        query_kernel,
        out_shape=jax.ShapeDtypeStruct((count_total, q_cols), jnp.float32),
        in_specs=[smem, *[VMEM] * 4],
        out_specs=VMEM,
        **settings(N_X - 1),
    )(where, held, query_own, query_right, query_left)
    attention, cache = pl.pallas_call(
        functools.partial(attend_kernel, head_size),
        out_shape=(
            jax.ShapeDtypeStruct((count_total, q_cols), jnp.bfloat16),
            jax.ShapeDtypeStruct((count_total, pair_width), jnp.bfloat16),
        ),
        in_specs=[smem, *[VMEM] * 10],
        out_specs=(VMEM, VMEM),
        **settings(1),
    )(where, held, query_far, near, partial, partner, q_gain[None], k_gain[None], cosine, sine, bias)
    return attention, cache[:, None, :]


def solution(mesh):
    fine = Mesh(
        mesh.devices.reshape(N_X, N_Z, N_YH, N_CORE, N_YL), ("x", "z", "yh", "core", "yl")
    )
    group, head = ("x", "z"), ("yh", "core")
    return jax.shard_map(
        body,
        mesh=fine,
        in_specs=(
            P((*group, *head, "yl"), None),
            P(group, (*head, "yl")),
            P((*group, "yl"), head, None),
            P(),
            P(),
            P(group, None),
        ),
        out_specs=(P(group, (*head, "yl")), P(group, head, None)),
        check_vma=False,
    )
```

```python
import functools
import math

import jax
import jax.numpy as jnp
from jax import lax
from jax.experimental import pallas as pl
from jax.experimental.pallas import tpu as pltpu
from jax.sharding import Mesh, PartitionSpec as P

QUERY_HEADS = 32
KEYVAL_HEADS = 8

theta_base = 1000000.0
epsilon = 1e-06

N_X, N_Z, N_YH, N_CORE, N_YL = 4, 16, 4, 2, 2
VMEM = pl.BlockSpec(memory_space=pltpu.VMEM)
HBM = pl.BlockSpec(memory_space=pltpu.HBM)


def token_places(seg_ids):
    count_total = seg_ids.shape[0]
    before = jnp.sum((seg_ids[None, :] < seg_ids[:, None]).astype(jnp.int32), axis=1)
    return jnp.arange(count_total, dtype=jnp.int32) - before


def norm_rotate(values, gain, cosine, sine):
    mean = jnp.mean(values * values, axis=-1, keepdims=True)
    values = values * lax.rsqrt(mean + epsilon) * gain
    return values * cosine + pltpu.roll(values, values.shape[-1] // 2, 1) * sine


def meet(where, held, steps, weight):
    rows = weight.reshape(-1, weight.shape[-1])
    wide = rows.shape[0]
    start = pl.multiple_of(lax.rem(where[0] + steps, N_X) * wide, wide)
    return jnp.dot(
        held[:, :, :, :, pl.ds(start, wide)].reshape(-1, wide), rows, preferred_element_type=jnp.float32
    )


def order_kernel(whole, held, sems):
    copies = [
        pltpu.make_async_copy(whole.at[:, near, core], held.at[:, core, near], sems.at[core, near])
        for core in range(N_CORE)
        for near in range(N_YL)
    ]
    for copy in copies:
        copy.start()
    for copy in copies:
        copy.wait()


def keyval_kernel(where, held, own, right, left, far, out, weight):
    rows = own.shape[1]
    for half in range(N_YL):

        @pl.when(where[1] == half)
        def _():
            away = (1 - half) * rows
            for n, ref in enumerate((own, left, far, right)):
                weight[n, :, half * rows : half * rows + rows, :] = ref[...]
                weight[n, :, away : away + rows, :] = jnp.zeros_like(ref)

    out[...] = sum(meet(where, held, n, weight[n]) for n in range(N_X))


def query_kernel(where, held, own, left, out):
    out[...] = meet(where, held, 0, own[...]) + meet(where, held, 1, left[...])


def attend_kernel(
    head_size, where, held, far, right, near, own, partner, q_gain, k_gain, cosine, sine, bias, out, cache
):
    query = near[...] + meet(where, held, N_X - 1, right[...]) + meet(where, held, 2, far[...])
    key_value = own[...] + partner[...]
    key_rot = norm_rotate(key_value[:, :head_size], k_gain[...], cosine[...], sine[...]).astype(jnp.bfloat16)
    value_b = key_value[:, head_size:].astype(jnp.bfloat16)
    cache[:, :head_size] = key_rot
    cache[:, head_size:] = value_b
    for h in range(out.shape[1] // head_size):
        span = slice(h * head_size, (h + 1) * head_size)
        query_rot = norm_rotate(query[:, span], q_gain[...], cosine[...], sine[...]).astype(jnp.bfloat16)
        scores = lax.dot_general(
            query_rot, key_rot, (((1,), (1,)), ((), ())), preferred_element_type=jnp.float32
        ) / math.sqrt(head_size)
        masked = scores + bias[...]
        expd = jnp.exp(masked - jnp.max(masked, axis=-1, keepdims=True))
        probs = (expd / jnp.sum(expd, axis=-1, keepdims=True)).astype(jnp.bfloat16)
        out[:, span] = jnp.dot(probs, value_b, preferred_element_type=jnp.float32).astype(jnp.bfloat16)


def body(tokens, w_query, keyval_weight, q_gain, k_gain, segments):
    q_rows, q_cols = w_query.shape
    kv_rows, _, pair_width = keyval_weight.shape
    head_size = pair_width // 2
    where = jnp.stack([lax.axis_index(axis) for axis in ("x", "yl")]).astype(jnp.int32)

    pair = lax.all_gather(tokens, "core", axis=0, tiled=True)
    whole = lax.all_gather(pair, ("yh", "yl"), axis=0, tiled=True)

    seg_ids = segments.reshape(-1)
    count_total = seg_ids.shape[0]
    half = head_size // 2
    freqs = jnp.power(theta_base, -2.0 * jnp.arange(half, dtype=jnp.float32) / head_size)
    angles = token_places(seg_ids).astype(jnp.float32)[:, None] * freqs[None, :]
    cosine, sine = jnp.cos(angles), jnp.sin(angles)
    cosine = jnp.concatenate([cosine, cosine], axis=1)
    sine = jnp.concatenate([-sine, sine], axis=1)

    index = jnp.arange(count_total, dtype=jnp.int32)
    allowed = (index[None, :] <= index[:, None]) & (seg_ids[None, :] == seg_ids[:, None])
    bias = jnp.where(allowed, jnp.float32(0.0), jnp.float32(-1e30))

    block = jnp.concatenate([w_query, keyval_weight.reshape(kv_rows, pair_width)], axis=0)
    column = lax.all_gather(block, "z", axis=0)
    def up(a):
        return lax.ppermute(a, "x", [(x, (x + 1) % N_X) for x in range(N_X)])

    def down(a):
        return lax.ppermute(a, "x", [(x, (x - 1) % N_X) for x in range(N_X)])

    query_own, key_own = column[:, :q_rows], column[:, q_rows:]
    query_left = down(query_own)
    key_own, where, cosine, sine = lax.optimization_barrier((key_own, where, cosine, sine))
    key_right, key_left = up(key_own), down(key_own)
    key_right, query_own, bias = lax.optimization_barrier((key_right, query_own, bias))
    query_right = up(query_own)
    key_far = up(key_right)
    whole, key_right = lax.optimization_barrier((whole, key_right))
    depth = N_X * N_Z * q_rows
    held = pl.pallas_call(
        order_kernel,
        out_shape=jax.ShapeDtypeStruct((N_YH, N_CORE, N_YL, tokens.shape[0], depth), jnp.bfloat16),
        in_specs=[HBM],
        out_specs=VMEM,
        scratch_shapes=[pltpu.SemaphoreType.DMA((N_CORE, N_YL))],
        cost_estimate=pl.CostEstimate(flops=0, bytes_accessed=10 * 4 * count_total * depth, transcendentals=0),
        compiler_params=pltpu.CompilerParams(vmem_limit_bytes=16 << 20),
    )(pltpu.with_memory_space_constraint(whole.reshape(N_YH, N_YL, N_CORE, tokens.shape[0], depth), pltpu.HBM))

    query_left, held = lax.optimization_barrier((query_left, held))
    query_far = down(query_left)
    smem = pl.BlockSpec(memory_space=pltpu.SMEM)

    def settings(slots):
        return dict(
            cost_estimate=pl.CostEstimate(
                flops=10 * 2 * slots * count_total * (depth // N_X) * q_cols,
                bytes_accessed=10 * 2 * slots * (depth // N_X) * (q_cols + count_total),
                transcendentals=0,
            ),
            compiler_params=pltpu.CompilerParams(vmem_limit_bytes=16 << 20),
        )

    partial = pl.pallas_call(
        keyval_kernel,
        out_shape=jax.ShapeDtypeStruct((count_total, pair_width), jnp.float32),
        in_specs=[smem, *[VMEM] * 5],
        out_specs=VMEM,
        scratch_shapes=[pltpu.VMEM((N_X, N_Z, q_rows, q_cols), jnp.bfloat16)],
        **settings(N_X),
    )(where, held, key_own, key_right, key_left, key_far)
    partner = lax.ppermute(partial, "yl", [(0, 1), (1, 0)])
    near = pl.pallas_call(
        query_kernel,
        out_shape=jax.ShapeDtypeStruct((count_total, q_cols), jnp.float32),
        in_specs=[smem, *[VMEM] * 3],
        out_specs=VMEM,
        **settings(2),
    )(where, held, query_own, query_left)
    attention, cache = pl.pallas_call(
        functools.partial(attend_kernel, head_size),
        out_shape=(
            jax.ShapeDtypeStruct((count_total, q_cols), jnp.bfloat16),
            jax.ShapeDtypeStruct((count_total, pair_width), jnp.bfloat16),
        ),
        in_specs=[smem, *[VMEM] * 11],
        out_specs=(VMEM, VMEM),
        **settings(2),
    )(where, held, query_far, query_right, near, partial, partner, q_gain[None], k_gain[None], cosine, sine, bias)
    return attention, cache[:, None, :]


def solution(mesh):
    fine = Mesh(
        mesh.devices.reshape(N_X, N_Z, N_YH, N_CORE, N_YL), ("x", "z", "yh", "core", "yl")
    )
    group, head = ("x", "z"), ("yh", "core")
    return jax.shard_map(
        body,
        mesh=fine,
        in_specs=(
            P((*group, *head, "yl"), None),
            P(group, (*head, "yl")),
            P((*group, "yl"), head, None),
            P(),
            P(),
            P(group, None),
        ),
        out_specs=(P(group, (*head, "yl")), P(group, head, None)),
        check_vma=False,
    )
```

```python
import functools
import math

import jax
import jax.numpy as jnp
from jax import lax
from jax.experimental import pallas as pl
from jax.experimental.pallas import tpu as pltpu
from jax.sharding import Mesh, PartitionSpec as P

QUERY_HEADS = 32
KEYVAL_HEADS = 8

theta_base = 1000000.0
epsilon = 1e-06

N_X, N_Z, N_YH, N_CORE, N_YL = 4, 16, 4, 2, 2
VMEM = pl.BlockSpec(memory_space=pltpu.VMEM)
HBM = pl.BlockSpec(memory_space=pltpu.HBM)


def token_places(seg_ids):
    count_total = seg_ids.shape[0]
    before = jnp.sum((seg_ids[None, :] < seg_ids[:, None]).astype(jnp.int32), axis=1)
    return jnp.arange(count_total, dtype=jnp.int32) - before


def norm_rotate(values, gain, cosine, sine):
    mean = jnp.mean(values * values, axis=-1, keepdims=True)
    values = values * lax.rsqrt(mean + epsilon) * gain
    return values * cosine + pltpu.roll(values, values.shape[-1] // 2, 1) * sine


def meet(where, held, steps, weight):
    rows = weight.reshape(-1, weight.shape[-1])
    wide = rows.shape[0]
    start = pl.multiple_of(lax.rem(where[0] + steps, N_X) * wide, wide)
    return jnp.dot(
        held[:, :, :, :, pl.ds(start, wide)].reshape(-1, wide), rows, preferred_element_type=jnp.float32
    )


def order_kernel(where, mine, other, held, sems):
    copies = [
        pltpu.make_async_copy(rows, held.at[:, core], sems.at[n])
        for n, (rows, core) in enumerate(((mine, where[2]), (other, 1 - where[2])))
    ]
    for copy in copies:
        copy.start()
    for copy in copies:
        copy.wait()


def keyval_kernel(where, held, own, right, left, far, out, weight):
    rows = own.shape[1]
    for half in range(N_YL):

        @pl.when(where[1] == half)
        def _():
            away = (1 - half) * rows
            for n, ref in enumerate((own, left, far, right)):
                weight[n, :, half * rows : half * rows + rows, :] = ref[...]
                weight[n, :, away : away + rows, :] = jnp.zeros_like(ref)

    out[...] = sum(meet(where, held, n, weight[n]) for n in range(N_X))


def query_kernel(where, held, own, left, out):
    out[...] = meet(where, held, 0, own[...]) + meet(where, held, 1, left[...])


def attend_kernel(
    head_size, where, held, far, right, near, own, partner, q_gain, k_gain, cosine, sine, bias, out, cache
):
    query = near[...] + meet(where, held, N_X - 1, right[...]) + meet(where, held, 2, far[...])
    key_value = own[...] + partner[...]
    key_rot = norm_rotate(key_value[:, :head_size], k_gain[...], cosine[...], sine[...]).astype(jnp.bfloat16)
    value_b = key_value[:, head_size:].astype(jnp.bfloat16)
    cache[:, :head_size] = key_rot
    cache[:, head_size:] = value_b
    for h in range(out.shape[1] // head_size):
        span = slice(h * head_size, (h + 1) * head_size)
        query_rot = norm_rotate(query[:, span], q_gain[...], cosine[...], sine[...]).astype(jnp.bfloat16)
        scores = lax.dot_general(
            query_rot, key_rot, (((1,), (1,)), ((), ())), preferred_element_type=jnp.float32
        ) / math.sqrt(head_size)
        masked = scores + bias[...]
        expd = jnp.exp(masked - jnp.max(masked, axis=-1, keepdims=True))
        probs = (expd / jnp.sum(expd, axis=-1, keepdims=True)).astype(jnp.bfloat16)
        out[:, span] = jnp.dot(probs, value_b, preferred_element_type=jnp.float32).astype(jnp.bfloat16)


def body(tokens, w_query, keyval_weight, q_gain, k_gain, segments):
    q_rows, q_cols = w_query.shape
    kv_rows, _, pair_width = keyval_weight.shape
    head_size = pair_width // 2
    where = jnp.stack([lax.axis_index(axis) for axis in ("x", "yl", "core")]).astype(jnp.int32)

    mine = lax.all_to_all(
        jnp.broadcast_to(tokens[None], (N_YH * N_YL, *tokens.shape)), ("yh", "yl"), split_axis=0, concat_axis=0
    )

    seg_ids = segments.reshape(-1)
    count_total = seg_ids.shape[0]
    half = head_size // 2
    freqs = jnp.power(theta_base, -2.0 * jnp.arange(half, dtype=jnp.float32) / head_size)
    angles = token_places(seg_ids).astype(jnp.float32)[:, None] * freqs[None, :]
    cosine, sine = jnp.cos(angles), jnp.sin(angles)
    cosine = jnp.concatenate([cosine, cosine], axis=1)
    sine = jnp.concatenate([-sine, sine], axis=1)

    index = jnp.arange(count_total, dtype=jnp.int32)
    allowed = (index[None, :] <= index[:, None]) & (seg_ids[None, :] == seg_ids[:, None])
    bias = jnp.where(allowed, jnp.float32(0.0), jnp.float32(-1e30))

    block = jnp.concatenate([w_query, keyval_weight.reshape(kv_rows, pair_width)], axis=0)
    column = lax.all_gather(block, "z", axis=0)
    def up(a):
        return lax.ppermute(a, "x", [(x, (x + 1) % N_X) for x in range(N_X)])

    def down(a):
        return lax.ppermute(a, "x", [(x, (x - 1) % N_X) for x in range(N_X)])

    query_own, key_own = column[:, :q_rows], column[:, q_rows:]
    query_left = down(query_own)
    key_own, where, cosine, sine = lax.optimization_barrier((key_own, where, cosine, sine))
    key_right, key_left = up(key_own), down(key_own)
    key_right, query_own, bias = lax.optimization_barrier((key_right, query_own, bias))
    query_right = up(query_own)
    key_far = up(key_right)
    other = lax.ppermute(mine, "core", [(0, 1), (1, 0)])
    depth = N_X * N_Z * q_rows
    mine, other = (
        a.reshape(N_YH, N_YL, tokens.shape[0], depth) for a in (mine, other)
    )
    smem = pl.BlockSpec(memory_space=pltpu.SMEM)
    held = pl.pallas_call(
        order_kernel,
        out_shape=jax.ShapeDtypeStruct((N_YH, N_CORE, N_YL, tokens.shape[0], depth), jnp.bfloat16),
        in_specs=[smem, VMEM, VMEM],
        out_specs=VMEM,
        scratch_shapes=[pltpu.SemaphoreType.DMA((N_CORE,))],
        cost_estimate=pl.CostEstimate(flops=0, bytes_accessed=10 * 4 * count_total * depth, transcendentals=0),
        compiler_params=pltpu.CompilerParams(vmem_limit_bytes=16 << 20),
    )(where, mine, other)
    query_left, held = lax.optimization_barrier((query_left, held))
    query_far = down(query_left)

    def settings(slots):
        return dict(
            cost_estimate=pl.CostEstimate(
                flops=10 * 2 * slots * count_total * (depth // N_X) * q_cols,
                bytes_accessed=10 * 2 * slots * (depth // N_X) * (q_cols + count_total),
                transcendentals=0,
            ),
            compiler_params=pltpu.CompilerParams(vmem_limit_bytes=16 << 20),
        )

    partial = pl.pallas_call(
        keyval_kernel,
        out_shape=jax.ShapeDtypeStruct((count_total, pair_width), jnp.float32),
        in_specs=[smem, *[VMEM] * 5],
        out_specs=VMEM,
        scratch_shapes=[pltpu.VMEM((N_X, N_Z, q_rows, q_cols), jnp.bfloat16)],
        **settings(N_X),
    )(where, held, key_own, key_right, key_left, key_far)
    partner = lax.ppermute(partial, "yl", [(0, 1), (1, 0)])
    near = pl.pallas_call(
        query_kernel,
        out_shape=jax.ShapeDtypeStruct((count_total, q_cols), jnp.float32),
        in_specs=[smem, *[VMEM] * 3],
        out_specs=VMEM,
        **settings(2),
    )(where, held, query_own, query_left)
    attention, cache = pl.pallas_call(
        functools.partial(attend_kernel, head_size),
        out_shape=(
            jax.ShapeDtypeStruct((count_total, q_cols), jnp.bfloat16),
            jax.ShapeDtypeStruct((count_total, pair_width), jnp.bfloat16),
        ),
        in_specs=[smem, *[VMEM] * 11],
        out_specs=(VMEM, VMEM),
        **settings(2),
    )(where, held, query_far, query_right, near, partial, partner, q_gain[None], k_gain[None], cosine, sine, bias)
    return attention, cache[:, None, :]


def solution(mesh):
    fine = Mesh(
        mesh.devices.reshape(N_X, N_Z, N_YH, N_CORE, N_YL), ("x", "z", "yh", "core", "yl")
    )
    group, head = ("x", "z"), ("yh", "core")
    return jax.shard_map(
        body,
        mesh=fine,
        in_specs=(
            P((*group, *head, "yl"), None),
            P(group, (*head, "yl")),
            P((*group, "yl"), head, None),
            P(),
            P(),
            P(group, None),
        ),
        out_specs=(P(group, (*head, "yl")), P(group, head, None)),
        check_vma=False,
    )
```

```python
import functools
import math

import jax
import jax.numpy as jnp
from jax import lax
from jax.experimental import pallas as pl
from jax.experimental.pallas import tpu as pltpu
from jax.sharding import Mesh, PartitionSpec as P

QUERY_HEADS = 32
KEYVAL_HEADS = 8

theta_base = 1000000.0
epsilon = 1e-06

N_X, N_Z, N_YH, N_CORE, N_YL = 4, 16, 4, 2, 2
VMEM = pl.BlockSpec(memory_space=pltpu.VMEM)
HBM = pl.BlockSpec(memory_space=pltpu.HBM)


def token_places(seg_ids):
    count_total = seg_ids.shape[0]
    before = jnp.sum((seg_ids[None, :] < seg_ids[:, None]).astype(jnp.int32), axis=1)
    return jnp.arange(count_total, dtype=jnp.int32) - before


def norm_rotate(values, gain, cosine, sine):
    mean = jnp.mean(values * values, axis=-1, keepdims=True)
    values = values * lax.rsqrt(mean + epsilon) * gain
    return values * cosine + pltpu.roll(values, values.shape[-1] // 2, 1) * sine


def meet(where, held, steps, weight):
    rows = weight.reshape(-1, weight.shape[-1])
    wide = rows.shape[0]
    start = pl.multiple_of(lax.rem(where[0] + steps, N_X) * wide, wide)
    return jnp.dot(
        held[:, :, :, :, pl.ds(start, wide)].reshape(-1, wide), rows, preferred_element_type=jnp.float32
    )


def order_kernel(where, mine, other, held, sems):
    copies = [
        pltpu.make_async_copy(rows, held.at[:, core], sems.at[n])
        for n, (rows, core) in enumerate(((mine, where[2]), (other, 1 - where[2])))
    ]
    for copy in copies:
        copy.start()
    for copy in copies:
        copy.wait()


def keyval_kernel(where, held, own, right, left, far, out, weight):
    rows = own.shape[1]
    for half in range(N_YL):

        @pl.when(where[1] == half)
        def _():
            away = (1 - half) * rows
            for n, ref in enumerate((own, left, far, right)):
                weight[n, :, half * rows : half * rows + rows, :] = ref[...]
                weight[n, :, away : away + rows, :] = jnp.zeros_like(ref)

    out[...] = sum(meet(where, held, n, weight[n]) for n in range(N_X))


def query_kernel(where, held, own, left, out):
    out[...] = meet(where, held, 0, own[...]) + meet(where, held, 1, left[...])


def attend_kernel(
    head_size, where, held, far, right, near, own, partner, q_gain, k_gain, cosine, sine, bias, out, cache
):
    query = near[...] + meet(where, held, N_X - 1, right[...]) + meet(where, held, 2, far[...])
    key_value = own[...] + partner[...]
    key_rot = norm_rotate(key_value[:, :head_size], k_gain[...], cosine[...], sine[...]).astype(jnp.bfloat16)
    value_b = key_value[:, head_size:].astype(jnp.bfloat16)
    cache[:, :head_size] = key_rot
    cache[:, head_size:] = value_b
    for h in range(out.shape[1] // head_size):
        span = slice(h * head_size, (h + 1) * head_size)
        query_rot = norm_rotate(query[:, span], q_gain[...], cosine[...], sine[...]).astype(jnp.bfloat16)
        scores = lax.dot_general(
            query_rot, key_rot, (((1,), (1,)), ((), ())), preferred_element_type=jnp.float32
        ) / math.sqrt(head_size)
        masked = scores + bias[...]
        expd = jnp.exp(masked - jnp.max(masked, axis=-1, keepdims=True))
        probs = (expd / jnp.sum(expd, axis=-1, keepdims=True)).astype(jnp.bfloat16)
        out[:, span] = jnp.dot(probs, value_b, preferred_element_type=jnp.float32).astype(jnp.bfloat16)


def body(tokens, w_query, keyval_weight, q_gain, k_gain, segments):
    q_rows, q_cols = w_query.shape
    kv_rows, _, pair_width = keyval_weight.shape
    head_size = pair_width // 2
    where = jnp.stack([lax.axis_index(axis) for axis in ("x", "yl", "core")]).astype(jnp.int32)

    mine = lax.all_to_all(
        jnp.broadcast_to(tokens[None], (N_YH * N_YL, *tokens.shape)), ("yh", "yl"), split_axis=0, concat_axis=0
    )

    seg_ids = segments.reshape(-1)
    count_total = seg_ids.shape[0]
    half = head_size // 2
    freqs = jnp.power(theta_base, -2.0 * jnp.arange(half, dtype=jnp.float32) / head_size)
    angles = token_places(seg_ids).astype(jnp.float32)[:, None] * freqs[None, :]
    cosine, sine = jnp.cos(angles), jnp.sin(angles)
    cosine = jnp.concatenate([cosine, cosine], axis=1)
    sine = jnp.concatenate([-sine, sine], axis=1)

    index = jnp.arange(count_total, dtype=jnp.int32)
    allowed = (index[None, :] <= index[:, None]) & (seg_ids[None, :] == seg_ids[:, None])
    bias = jnp.where(allowed, jnp.float32(0.0), jnp.float32(-1e30))

    block = jnp.concatenate([w_query, keyval_weight.reshape(kv_rows, pair_width)], axis=0)
    column = lax.all_gather(block, "z", axis=0)
    def up(a):
        return lax.ppermute(a, "x", [(x, (x + 1) % N_X) for x in range(N_X)])

    def down(a):
        return lax.ppermute(a, "x", [(x, (x - 1) % N_X) for x in range(N_X)])

    query_own, key_own = column[:, :q_rows], column[:, q_rows:]
    query_own, where = lax.optimization_barrier((query_own, where))
    query_left = down(query_own)
    key_right, key_left = up(key_own), down(key_own)
    key_right, query_own, cosine, sine, bias = lax.optimization_barrier((key_right, query_own, cosine, sine, bias))
    query_right = up(query_own)
    key_far = up(key_right)
    mine, key_own = lax.optimization_barrier((mine, key_own))
    other = lax.ppermute(mine, "core", [(0, 1), (1, 0)])
    depth = N_X * N_Z * q_rows
    mine, other = (
        a.reshape(N_YH, N_YL, tokens.shape[0], depth) for a in (mine, other)
    )
    smem = pl.BlockSpec(memory_space=pltpu.SMEM)
    held = pl.pallas_call(
        order_kernel,
        out_shape=jax.ShapeDtypeStruct((N_YH, N_CORE, N_YL, tokens.shape[0], depth), jnp.bfloat16),
        in_specs=[smem, VMEM, VMEM],
        out_specs=VMEM,
        scratch_shapes=[pltpu.SemaphoreType.DMA((N_CORE,))],
        cost_estimate=pl.CostEstimate(flops=0, bytes_accessed=10 * 4 * count_total * depth, transcendentals=0),
        compiler_params=pltpu.CompilerParams(vmem_limit_bytes=16 << 20),
    )(where, mine, other)
    query_left, held = lax.optimization_barrier((query_left, held))
    query_far = down(query_left)

    def settings(slots):
        return dict(
            cost_estimate=pl.CostEstimate(
                flops=10 * 2 * slots * count_total * (depth // N_X) * q_cols,
                bytes_accessed=10 * 2 * slots * (depth // N_X) * (q_cols + count_total),
                transcendentals=0,
            ),
            compiler_params=pltpu.CompilerParams(vmem_limit_bytes=16 << 20),
        )

    partial = pl.pallas_call(
        keyval_kernel,
        out_shape=jax.ShapeDtypeStruct((count_total, pair_width), jnp.float32),
        in_specs=[smem, *[VMEM] * 5],
        out_specs=VMEM,
        scratch_shapes=[pltpu.VMEM((N_X, N_Z, q_rows, q_cols), jnp.bfloat16)],
        **settings(N_X),
    )(where, held, key_own, key_right, key_left, key_far)
    partner = lax.ppermute(partial, "yl", [(0, 1), (1, 0)])
    near = pl.pallas_call(
        query_kernel,
        out_shape=jax.ShapeDtypeStruct((count_total, q_cols), jnp.float32),
        in_specs=[smem, *[VMEM] * 3],
        out_specs=VMEM,
        **settings(2),
    )(where, held, query_own, query_left)
    attention, cache = pl.pallas_call(
        functools.partial(attend_kernel, head_size),
        out_shape=(
            jax.ShapeDtypeStruct((count_total, q_cols), jnp.bfloat16),
            jax.ShapeDtypeStruct((count_total, pair_width), jnp.bfloat16),
        ),
        in_specs=[smem, *[VMEM] * 11],
        out_specs=(VMEM, VMEM),
        **settings(2),
    )(where, held, query_far, query_right, near, partial, partner, q_gain[None], k_gain[None], cosine, sine, bias)
    return attention, cache[:, None, :]


def solution(mesh):
    fine = Mesh(
        mesh.devices.reshape(N_X, N_Z, N_YH, N_CORE, N_YL), ("x", "z", "yh", "core", "yl")
    )
    group, head = ("x", "z"), ("yh", "core")
    return jax.shard_map(
        body,
        mesh=fine,
        in_specs=(
            P((*group, *head, "yl"), None),
            P(group, (*head, "yl")),
            P((*group, "yl"), head, None),
            P(),
            P(),
            P(group, None),
        ),
        out_specs=(P(group, (*head, "yl")), P(group, head, None)),
        check_vma=False,
    )
```

```python
import functools
import math

import jax
import jax.numpy as jnp
from jax import lax
from jax.experimental import pallas as pl
from jax.experimental.pallas import tpu as pltpu
from jax.sharding import Mesh, PartitionSpec as P

QUERY_HEADS = 32
KEYVAL_HEADS = 8

theta_base = 1000000.0
epsilon = 1e-06

N_X, N_Z, N_YH, N_CORE, N_YL = 4, 16, 4, 2, 2
VMEM = pl.BlockSpec(memory_space=pltpu.VMEM)
HBM = pl.BlockSpec(memory_space=pltpu.HBM)


def token_places(seg_ids):
    count_total = seg_ids.shape[0]
    before = jnp.sum((seg_ids[None, :] < seg_ids[:, None]).astype(jnp.int32), axis=1)
    return jnp.arange(count_total, dtype=jnp.int32) - before


def norm_rotate(values, gain, cosine, sine):
    mean = jnp.mean(values * values, axis=-1, keepdims=True)
    values = values * lax.rsqrt(mean + epsilon) * gain
    return values * cosine + pltpu.roll(values, values.shape[-1] // 2, 1) * sine


def meet(where, held, steps, weight):
    rows = weight.reshape(-1, weight.shape[-1])
    wide = rows.shape[0]
    start = pl.multiple_of(lax.rem(where[0] + steps, N_X) * wide, wide)
    return jnp.dot(
        held[:, :, :, :, pl.ds(start, wide)].reshape(-1, wide), rows, preferred_element_type=jnp.float32
    )


def order_kernel(where, mine, other, held, sems):
    copies = [
        pltpu.make_async_copy(rows, held.at[:, core], sems.at[n])
        for n, (rows, core) in enumerate(((mine, where[2]), (other, 1 - where[2])))
    ]
    for copy in copies:
        copy.start()
    for copy in copies:
        copy.wait()


def keyval_kernel(where, held, own, right, left, far, out, weight):
    rows = own.shape[1]
    for half in range(N_YL):

        @pl.when(where[1] == half)
        def _():
            away = (1 - half) * rows
            for n, ref in enumerate((own, left, far, right)):
                weight[n, :, half * rows : half * rows + rows, :] = ref[...]
                weight[n, :, away : away + rows, :] = jnp.zeros_like(ref)

    out[...] = sum(meet(where, held, n, weight[n]) for n in range(N_X))


def query_kernel(where, held, own, left, out):
    out[...] = meet(where, held, 0, own[...]) + meet(where, held, 1, left[...])


def attend_kernel(
    head_size, where, held, far, right, near, own, partner, q_gain, k_gain, cosine, sine, bias, out, cache
):
    query = near[...] + meet(where, held, N_X - 1, right[...]) + meet(where, held, 2, far[...])
    key_value = own[...] + partner[...]
    key_rot = norm_rotate(key_value[:, :head_size], k_gain[...], cosine[...], sine[...]).astype(jnp.bfloat16)
    value_b = key_value[:, head_size:].astype(jnp.bfloat16)
    cache[:, :head_size] = key_rot
    cache[:, head_size:] = value_b
    for h in range(out.shape[1] // head_size):
        span = slice(h * head_size, (h + 1) * head_size)
        query_rot = norm_rotate(query[:, span], q_gain[...], cosine[...], sine[...]).astype(jnp.bfloat16)
        scores = lax.dot_general(
            query_rot, key_rot, (((1,), (1,)), ((), ())), preferred_element_type=jnp.float32
        ) / math.sqrt(head_size)
        masked = scores + bias[...]
        expd = jnp.exp(masked - jnp.max(masked, axis=-1, keepdims=True))
        probs = (expd / jnp.sum(expd, axis=-1, keepdims=True)).astype(jnp.bfloat16)
        out[:, span] = jnp.dot(probs, value_b, preferred_element_type=jnp.float32).astype(jnp.bfloat16)


def body(tokens, w_query, keyval_weight, q_gain, k_gain, segments):
    q_rows, q_cols = w_query.shape
    kv_rows, _, pair_width = keyval_weight.shape
    head_size = pair_width // 2
    where = jnp.stack([lax.axis_index(axis) for axis in ("x", "yl", "core")]).astype(jnp.int32)

    mine = lax.all_to_all(
        jnp.broadcast_to(tokens[None], (N_YH * N_YL, *tokens.shape)), ("yh", "yl"), split_axis=0, concat_axis=0
    )

    seg_ids = segments.reshape(-1)
    count_total = seg_ids.shape[0]
    half = head_size // 2
    freqs = jnp.power(theta_base, -2.0 * jnp.arange(half, dtype=jnp.float32) / head_size)
    angles = token_places(seg_ids).astype(jnp.float32)[:, None] * freqs[None, :]
    cosine, sine = jnp.cos(angles), jnp.sin(angles)
    cosine = jnp.concatenate([cosine, cosine], axis=1)
    sine = jnp.concatenate([-sine, sine], axis=1)

    index = jnp.arange(count_total, dtype=jnp.int32)
    allowed = (index[None, :] <= index[:, None]) & (seg_ids[None, :] == seg_ids[:, None])
    bias = jnp.where(allowed, jnp.float32(0.0), jnp.float32(-1e30))

    block = jnp.concatenate([w_query, keyval_weight.reshape(kv_rows, pair_width)], axis=0)
    column = lax.all_gather(block, "z", axis=0)
    def up(a):
        return lax.ppermute(a, "x", [(x, (x + 1) % N_X) for x in range(N_X)])

    def down(a):
        return lax.ppermute(a, "x", [(x, (x - 1) % N_X) for x in range(N_X)])

    query_own, key_own = column[:, :q_rows], column[:, q_rows:]
    query_own, where = lax.optimization_barrier((query_own, where))
    key_right, query_left = up(key_own), down(query_own)
    key_last, cosine, sine = lax.optimization_barrier((key_own, cosine, sine))
    key_left = down(key_last)
    key_right, query_last, bias = lax.optimization_barrier((key_right, query_own, bias))
    query_right = up(query_last)
    key_far = up(key_right)
    mine, key_own = lax.optimization_barrier((mine, key_own))
    other = lax.ppermute(mine, "core", [(0, 1), (1, 0)])
    depth = N_X * N_Z * q_rows
    mine, other = (
        a.reshape(N_YH, N_YL, tokens.shape[0], depth) for a in (mine, other)
    )
    smem = pl.BlockSpec(memory_space=pltpu.SMEM)
    held = pl.pallas_call(
        order_kernel,
        out_shape=jax.ShapeDtypeStruct((N_YH, N_CORE, N_YL, tokens.shape[0], depth), jnp.bfloat16),
        in_specs=[smem, VMEM, VMEM],
        out_specs=VMEM,
        scratch_shapes=[pltpu.SemaphoreType.DMA((N_CORE,))],
        cost_estimate=pl.CostEstimate(flops=0, bytes_accessed=10 * 4 * count_total * depth, transcendentals=0),
        compiler_params=pltpu.CompilerParams(vmem_limit_bytes=16 << 20),
    )(where, mine, other)
    query_left, held = lax.optimization_barrier((query_left, held))
    query_far = down(query_left)

    def settings(slots):
        return dict(
            cost_estimate=pl.CostEstimate(
                flops=10 * 2 * slots * count_total * (depth // N_X) * q_cols,
                bytes_accessed=10 * 2 * slots * (depth // N_X) * (q_cols + count_total),
                transcendentals=0,
            ),
            compiler_params=pltpu.CompilerParams(vmem_limit_bytes=16 << 20),
        )

    partial = pl.pallas_call(
        keyval_kernel,
        out_shape=jax.ShapeDtypeStruct((count_total, pair_width), jnp.float32),
        in_specs=[smem, *[VMEM] * 5],
        out_specs=VMEM,
        scratch_shapes=[pltpu.VMEM((N_X, N_Z, q_rows, q_cols), jnp.bfloat16)],
        **settings(N_X),
    )(where, held, key_own, key_right, key_left, key_far)
    partner = lax.ppermute(partial, "yl", [(0, 1), (1, 0)])
    near = pl.pallas_call(
        query_kernel,
        out_shape=jax.ShapeDtypeStruct((count_total, q_cols), jnp.float32),
        in_specs=[smem, *[VMEM] * 3],
        out_specs=VMEM,
        **settings(2),
    )(where, held, query_own, query_left)
    attention, cache = pl.pallas_call(
        functools.partial(attend_kernel, head_size),
        out_shape=(
            jax.ShapeDtypeStruct((count_total, q_cols), jnp.bfloat16),
            jax.ShapeDtypeStruct((count_total, pair_width), jnp.bfloat16),
        ),
        in_specs=[smem, *[VMEM] * 11],
        out_specs=(VMEM, VMEM),
        **settings(2),
    )(where, held, query_far, query_right, near, partial, partner, q_gain[None], k_gain[None], cosine, sine, bias)
    return attention, cache[:, None, :]


def solution(mesh):
    fine = Mesh(
        mesh.devices.reshape(N_X, N_Z, N_YH, N_CORE, N_YL), ("x", "z", "yh", "core", "yl")
    )
    group, head = ("x", "z"), ("yh", "core")
    return jax.shard_map(
        body,
        mesh=fine,
        in_specs=(
            P((*group, *head, "yl"), None),
            P(group, (*head, "yl")),
            P((*group, "yl"), head, None),
            P(),
            P(),
            P(group, None),
        ),
        out_specs=(P(group, (*head, "yl")), P(group, head, None)),
        check_vma=False,
    )
```
